128 devices in a mesh: ia: 8 (over y, core), ja: 16 (over x, z).
Axes of the slice: x: 4, y: 4, z: 4, core: 2. Of those that a mesh axis runs over, the one named last changes fastest.
Arguments:
- amplitudes: bfloat16 [1024, 128, 128], P(('ia', 'ja')), may hold values from -6 to 6
- bases: bfloat16 [1024, 512, 128], P(('ia', 'ja')), may hold values from -1 to 1
- exchange_ints: bfloat16 [1024, 128, 128], P(('ia', 'ja')), may hold values from -6 to 6
- cycle_ints: bfloat16 [1024, 32, 128, 128], P(('ia', 'ja')), may hold values from -0.0625 to 0.0625
- pno_energy: float32 [1024, 128], P(('ia', 'ja')), may hold values from 0.2 to 3
- occ_energy: float32 [1024], P(('ia', 'ja')), may hold values from -1.5 to -0.3
- pno_count: int32 [1024], P(('ia', 'ja')), may hold values from 32 to 128, as said below
- coupling: int32 [1024, 32], P(('ia', 'ja')), may hold values from 0 to 1023, as said below
- reverse: int32 [1024], P(('ia', 'ja')), may hold values from 0 to 1023, as said below
Outputs:
- new_amplitudes: bfloat16 [1024, 128, 128], P(('ia', 'ja'))
- residual: float32 [1024, 128, 128], P(('ia', 'ja'))
The draws below stay inside these ranges and needn't reach their ends.
Inputs may be any that keep to these rules, and one draw needn't show every extreme that they name: `coupling`: pair p is owned by the device at linear index p // 8 of the mesh (ia slowest). Over the 8 pairs of one device, the lists have exactly 2 entries that name pairs of each device (the device itself included), and these name exactly 1 distinct pairs of that device. `reverse`: reversal is an involution without fixed points; the reversed pair of a pair owned by the device at ja index b lies on the device with the same ia index and ja index b + 8 modulo 2 * 8. `pno_count`: some pair keeps all 128 natural orbitals.
All inputs are finite; a program needn't handle non-finite values.
Results may differ from the reference program's by a relative error of at most 0.0061.
Values may be sent and summed in bfloat16 or wider, within the bound.
No kernel may reach another device: no remote copies, remote signals or barrier semaphores. Data moves between devices by JAX's collectives and lax.ppermute only.
A program may use at most 192 MiB of HBM per device.

```python
import math
import jax
import jax.numpy as jnp
from jax import lax

NPNO = 128
DOMAIN = 512
PAIR_DEV = 8
COUPLE = 32
NPAIRS = 1024
CAP = 1
HALF_JA = 8


def shuffled(branch_key):
    return jax.random.permutation(branch_key, PAIR_DEV)


def draw_coupling(key, part):
    devices = NPAIRS // PAIR_DEV
    per_owner = 2 * CAP
    entries = PAIR_DEV * COUPLE

    def one_reader(reader_key):
        pieces = jax.random.split(reader_key, 3)
        orders = jax.vmap(shuffled)(jax.random.split(pieces[0], devices))
        chosen = orders[:, :CAP]
        extra = jax.random.randint(pieces[1], (devices, per_owner - CAP), 0, CAP)
        picks = jnp.concatenate([chosen, jnp.take_along_axis(chosen, extra, axis=1)], axis=1)
        owners = jnp.arange(devices, dtype=jnp.int32)[:, None]
        labels = (owners * PAIR_DEV + picks).reshape(-1)
        mixing = jax.random.permutation(pieces[2], entries)
        return labels[mixing].reshape(PAIR_DEV, COUPLE)
    readers = jax.vmap(one_reader)(jax.random.split(jax.random.fold_in(key, 11), devices))
    return readers.reshape(NPAIRS, COUPLE).astype(jnp.int32)


def draw_reverse(key, part):
    devices = NPAIRS // PAIR_DEV
    orders = jax.vmap(shuffled)(jax.random.split(jax.random.fold_in(key, 23), devices))
    device_ids = jnp.arange(devices, dtype=jnp.int32)
    partner = jnp.bitwise_xor(device_ids, HALF_JA)
    lower = device_ids // HALF_JA % 2 == 0
    inverse = jnp.argsort(orders, axis=1)
    slots = jnp.where(lower[:, None], orders, inverse[partner])
    result = partner[:, None] * PAIR_DEV + slots
    return result.reshape(NPAIRS).astype(jnp.int32)


def draw_pno_count(key, part):
    counts = jax.random.randint(jax.random.fold_in(key, 5), (NPAIRS,), NPNO // 4, NPNO + 1)
    chosen = jax.random.randint(jax.random.fold_in(key, 6), (), 0, NPAIRS)
    return jnp.where(jnp.arange(NPAIRS) == chosen, NPNO, counts).astype(jnp.int32)


def level_of(rng, dims, cuts, smallest, largest):
    gain = 1.0
    for dim, blocks in cuts:
        steps = jax.random.uniform(jax.random.fold_in(jax.random.fold_in(rng, 6), dim), (blocks,), jnp.float32, smallest / len(cuts), largest / len(cuts))
        gain = gain * jnp.repeat(jnp.exp(steps), dims[dim] // blocks).reshape((-1,) + (1,) * (len(dims) - 1 - dim))
    return gain


def normal_values(own_key, dims, width, most, cuts=(), kind=jnp.bfloat16):
    loudness = level_of(own_key, dims, cuts, -0.22, 0.18) if cuts else 1.0
    values = jax.random.normal(own_key, dims, jnp.float32) * width * loudness
    return jnp.minimum(jnp.maximum(values, -most), most).astype(kind)


def setup_inputs(seed: int = 0) -> dict:
    splits = jax.random.split(jax.random.key(seed), 10)
    return {
        "amplitudes": normal_values(splits[0], (NPAIRS, NPNO, NPNO), 1.0, 6.0, ((0, 128),)),
        "bases": normal_values(splits[1], (NPAIRS, DOMAIN, NPNO), ((DOMAIN * NPNO) ** -0.25), 1.0, ((0, 128),)),
        "exchange_ints": normal_values(splits[2], (NPAIRS, NPNO, NPNO), 1.0, 6.0, ((0, 128),)),
        "cycle_ints": normal_values(splits[3], (NPAIRS, COUPLE, NPNO, NPNO), (2 * COUPLE * NPNO) ** -0.5, 0.0625, ((0, 128),)),
        "pno_energy": jnp.clip(jnp.exp(math.log(3.0) - 2.7080502 * jax.random.uniform(splits[4], (NPAIRS, NPNO), jnp.float32) ** level_of(splits[4], (NPAIRS, NPNO), ((0, 128),), -0.2, 0.2)), 0.2, 3.0),
        "occ_energy": jnp.clip(-1.5 + 1.2 * jax.random.uniform(splits[5], (NPAIRS,), jnp.float32) ** level_of(splits[5], (NPAIRS,), ((0, 128),), -0.2, 0.2), -1.5, -0.3),
        "pno_count": draw_pno_count(jax.random.fold_in(splits[9], 71), 0),
        "coupling": draw_coupling(jax.random.fold_in(splits[9], 71), 0),
        "reverse": draw_reverse(jax.random.fold_in(splits[9], 71), 0),
    }


def rounded(values):
    return lax.optimization_barrier(values.astype(jnp.bfloat16)).astype(jnp.float32)


def reference(amplitudes, bases, exchange_ints, cycle_ints, pno_energy, occ_energy, pno_count, coupling, reverse):
    keep = (jnp.arange(NPNO, dtype=jnp.int32)[None, :] < pno_count[:, None]).astype(jnp.float32)
    keep_square = keep[:, :, None] * keep[:, None, :]
    amps_masked = (amplitudes.astype(jnp.float32) * keep_square).astype(jnp.bfloat16)
    bases_masked = (bases.astype(jnp.float32) * keep[:, None, :]).astype(jnp.bfloat16)

    def one_pair(inputs):
        own_basis, partners, cycle_block = inputs
        other_bases = bases_masked[partners].astype(jnp.float32)
        other_amps = amps_masked[partners].astype(jnp.float32)
        intersection = rounded(jnp.einsum("av,kaw->kvw", own_basis.astype(jnp.float32), other_bases))
        projected = rounded(jnp.einsum("kvw,kwu->kvu", intersection, other_amps))
        transformed = rounded(jnp.einsum("kvu,kxu->kvx", projected, intersection))
        cycle = cycle_block.astype(jnp.float32)
        total = jnp.einsum("kvw,kwu->vu", cycle, transformed) + jnp.einsum("kvw,kuw->vu", transformed, cycle)
        return total.astype(jnp.bfloat16)

    cycle_sum = lax.map(one_pair, (bases_masked, coupling, cycle_ints))
    mirrored = jnp.transpose(cycle_sum[reverse].astype(jnp.float32), (0, 2, 1))
    residual = (exchange_ints.astype(jnp.float32) + cycle_sum.astype(jnp.float32) + mirrored) * keep_square
    denominator = pno_energy[:, :, None] + pno_energy[:, None, :] - occ_energy[:, None, None]
    updated = (amps_masked.astype(jnp.float32) - residual / denominator) * keep_square
    return updated.astype(jnp.bfloat16), residual
```

```python
import functools

import jax
import jax.numpy as jnp
from jax import lax
from jax.experimental import pallas as pl
from jax.experimental.pallas import tpu as pltpu
from jax.sharding import PartitionSpec as P


RING = 4
AXES = ("ia", "ja")
CHUNKS = (
    ((0, 0), (0, 1), (0, 2), (0, 3)),
    ((3, 0), (3, 3), (1, 0), (1, 1)),
    ((3, 1), (3, 2), (1, 2), (1, 3)),
    ((2, 0), (2, 1), (2, 2), (2, 3)),
)
NT = (((1,), (1,)), ((), ()))


def ring_perm(stage, shift):
    pairs = []
    for i in range(2 * RING):
        for x in range(RING):
            for z in range(RING):
                if (i % 2 == 0) == (stage == 1):
                    there = (x + shift) % RING * RING + z
                else:
                    there = x * RING + (z + shift) % RING
                pairs.append((i * RING * RING + x * RING + z, i * RING * RING + there))
    return pairs


def shift_ja(value, stage, shift):
    return lax.ppermute(value, AXES, ring_perm(stage, shift))


def shift_ia(value, steps, flip):
    size = 2 * RING
    return lax.ppermute(
        value, "ia", [(i, (i // 2 + steps) % RING * 2 + (i % 2 ^ flip)) for i in range(size)]
    )


def owner_ja(core, x, z, u, t):
    dx = jnp.where(core == 0, t, u)
    dz = jnp.where(core == 0, u, t)
    return ((x + dx) & 3) * RING + ((z + dz) & 3)


def transform_kernel(chunk, codes, me, *refs):
    blocks, lines = refs[:4], refs[4:12]
    outs = refs[12:20]
    line_buf, result, sems = refs[20:]
    width = outs[0].shape[-1]
    depth = blocks[0].shape[1] - width
    i, j = me[0], me[1]
    y, core = i >> 1, i & 1
    x, z = j >> 2, j & 3

    pltpu.make_async_copy(lines[0], line_buf.at[0], sems.at[0]).start()

    def reader(r, carry):
        slot = r & 1
        for k in range(1, 8):

            @pl.when(r + 1 == k)
            def _():
                pltpu.make_async_copy(lines[k], line_buf.at[k & 1], sems.at[k & 1]).start()

        pltpu.make_async_copy(lines[0], line_buf.at[slot], sems.at[slot]).wait()
        there = ((y + (r & 3)) & 3) * 2 + (core ^ (r >> 2))
        for n, (u, t) in enumerate(chunk):
            code = codes[there * 16 + owner_ja(core, x, z, u, t)]
            q = code & 7
            first, second = (code >> 3) & 7, code >> 6
            mine = jnp.concatenate([line_buf[slot, first], line_buf[slot, second]], axis=0)
            inter = jnp.dot(
                mine, blocks[n][q, :depth], preferred_element_type=jnp.float32
            ).astype(jnp.bfloat16)
            proj = jnp.dot(
                inter, blocks[n][q, depth:], preferred_element_type=jnp.float32
            ).astype(jnp.bfloat16)
            for h in range(2):
                rows = slice(h * width, (h + 1) * width)
                result[n, h] = lax.dot_general(
                    proj[rows], inter[rows], NT, preferred_element_type=jnp.float32
                ).astype(jnp.bfloat16)
        for k in range(8):

            @pl.when(r == k)
            def _():
                outs[k][...] = result[...]

        return carry

    lax.fori_loop(0, 8, reader, 0)


def transform(chunk, codes, me, blocks, lines):
    pairs, depth, width = blocks[0].shape
    smem = pl.BlockSpec(memory_space=pltpu.SMEM)
    vmem = pl.BlockSpec(memory_space=pltpu.VMEM)
    hbm = pl.BlockSpec(memory_space=pl.ANY)
    out = jax.ShapeDtypeStruct((len(chunk), 2, width, width), jnp.bfloat16)
    flops = 64 * 2 * width * width * (depth + width)
    return pl.pallas_call(
        functools.partial(transform_kernel, chunk),
        out_shape=[out] * 8,
        in_specs=[smem, smem] + [vmem] * 4 + [hbm] * 8,
        out_specs=[vmem] * 8,
        scratch_shapes=[
            pltpu.VMEM((2,) + lines[0].shape, jnp.bfloat16),
            pltpu.VMEM((len(chunk), 2, width, width), jnp.bfloat16),
            pltpu.SemaphoreType.DMA((2,)),
        ],
        compiler_params=pltpu.CompilerParams(vmem_limit_bytes=40 << 20),
        cost_estimate=pl.CostEstimate(
            flops=4 * flops, bytes_accessed=16 << 20, transcendentals=0
        ),
        name="transform",
    )(codes, me, *blocks, *lines)


def cycle_kernel(chunk, spots, me, cycle, *refs):
    arrived, before, total = refs[:8], refs[8], refs[9]
    i, j = me[0], me[1]
    y, core = i >> 1, i & 1
    x, z = j >> 2, j & 3
    total[...] = before[...]
    for r in range(8):
        other = core ^ (r >> 2)
        worker = ((y - (r & 3)) & 3) * 2 + other
        for n, (u, t) in enumerate(chunk):
            owner = worker * 16 + owner_ja(other, x, z, u, t)
            for h in range(2):
                spot = spots[owner * 2 + h]
                block = cycle[spot]
                value = arrived[r][n, h]
                part = jnp.dot(block, value, preferred_element_type=jnp.float32)
                part += lax.dot_general(value, block, NT, preferred_element_type=jnp.float32)
                total[spot >> 5] += part


def cycle_part(chunk, spots, me, cycle, arrived, before):
    smem = pl.BlockSpec(memory_space=pltpu.SMEM)
    vmem = pl.BlockSpec(memory_space=pltpu.VMEM)
    width = cycle.shape[-1]
    return pl.pallas_call(
        functools.partial(cycle_kernel, chunk),
        out_shape=jax.ShapeDtypeStruct(before.shape, before.dtype),
        in_specs=[smem, smem] + [vmem] * 10,
        out_specs=vmem,
        compiler_params=pltpu.CompilerParams(vmem_limit_bytes=40 << 20),
        cost_estimate=pl.CostEstimate(
            flops=4 * 64 * 4 * width**3, bytes_accessed=11 << 20, transcendentals=0
        ),
        name="cycle",
    )(spots, me, cycle, *arrived, before)


def finish_kernel(rev, count, occ, exchange, amps, own, partner, energy, new, res):
    pairs, width = amps.shape[0], amps.shape[1]
    row = lax.broadcasted_iota(jnp.int32, (width, width), 0)
    col = lax.broadcasted_iota(jnp.int32, (width, width), 1)
    for p in range(pairs):
        keep = (row < count[p]) & (col < count[p])
        mirrored = partner[rev[p]].astype(jnp.float32).T
        total = exchange[p].astype(jnp.float32) + own[p].astype(jnp.float32) + mirrored
        total = jnp.where(keep, total, 0.0)
        across = jnp.broadcast_to(energy[pl.ds(p, 1), :], (width, width))
        below = across.T + across - occ[p]
        res[p] = total
        updated = amps[p].astype(jnp.float32) - total / below
        new[p] = jnp.where(keep, updated, 0.0).astype(jnp.bfloat16)


def finish(rev, count, occ, exchange, amps, own, partner, energy):
    smem = pl.BlockSpec(memory_space=pltpu.SMEM)
    vmem = pl.BlockSpec(memory_space=pltpu.VMEM)
    return pl.pallas_call(
        finish_kernel,
        out_shape=(
            jax.ShapeDtypeStruct(amps.shape, jnp.bfloat16),
            jax.ShapeDtypeStruct(amps.shape, jnp.float32),
        ),
        in_specs=[smem] * 3 + [vmem] * 5,
        out_specs=(vmem, vmem),
        name="finish",
    )(rev, count, occ, exchange, amps, own, partner, energy)


def local(
    amplitudes,
    bases,
    exchange_ints,
    cycle_ints,
    pno_energy,
    occ_energy,
    pno_count,
    coupling,
    reverse,
):
    pairs, width = amplitudes.shape[0], amplitudes.shape[1]
    couple = coupling.shape[1]
    devices = lax.axis_size("ia") * lax.axis_size("ja")
    me = jnp.stack([lax.axis_index("ia"), lax.axis_index("ja")]).astype(jnp.int32)
    keep = lax.broadcasted_iota(jnp.int32, (pairs, width), 1) < pno_count[:, None]
    keep_square = keep[:, :, None] & keep[:, None, :]
    amps_masked = jnp.where(keep_square, amplitudes, jnp.zeros_like(amplitudes))
    bases_masked = jnp.where(keep[:, None, :], bases, jnp.zeros_like(bases))
    block = jnp.concatenate([bases_masked, amps_masked], axis=1)
    line = jnp.transpose(bases_masked, (0, 2, 1))

    first = {0: block}
    first[3] = shift_ja(block, 1, 1)
    first[1] = shift_ja(block, 1, -1)
    first[2] = shift_ja(block, 1, 2)
    held = {(0, t): first[t] for t in range(RING)}
    for t in (0, 3, 1, 2):
        held[3, t] = shift_ja(first[t], 2, 1)
    for t in (0, 1, 2, 3):
        held[1, t] = shift_ja(first[t], 2, -1)
    for t in (0, 3):
        held[2, t] = shift_ja(held[3, t], 2, 1)
    for t in (1, 2):
        held[2, t] = shift_ja(held[1, t], 2, -1)

    lines = [line, shift_ia(line, -1, 0), shift_ia(line, 2, 0), shift_ia(line, 1, 0)]
    lines = lines + [shift_ia(value, 0, 1) for value in lines]

    entries = coupling.reshape(-1)
    owners = entries // pairs
    order = jnp.arange(entries.shape[0], dtype=jnp.int32)
    earlier = (owners[:, None] == owners[None, :]) & (order[:, None] < order[None, :])
    later = jnp.any(earlier, axis=0)
    named = owners[:, None] == jnp.arange(devices, dtype=jnp.int32)[None, :]
    heads = named & ~later[:, None]
    tails = named & later[:, None]
    spot_head = jnp.sum(jnp.where(heads, order[:, None], 0), axis=0)
    spot_tail = jnp.sum(jnp.where(tails, order[:, None], 0), axis=0)
    pair_named = jnp.sum(jnp.where(heads, (entries % pairs)[:, None], 0), axis=0)
    code = pair_named + spot_head // couple * 8 + spot_tail // couple * 64
    spots = jnp.stack([spot_head, spot_tail], axis=1).reshape(-1)
    codes = lax.all_to_all(
        code.reshape(lax.axis_size("ia"), -1), "ia", split_axis=0, concat_axis=0, tiled=True
    ).reshape(-1)

    cycle = cycle_ints.reshape(pairs * couple, width, width)
    total = jnp.zeros((pairs, width, width), jnp.float32)
    for chunk in CHUNKS:
        sent = transform(chunk, codes, me, [held[key] for key in chunk], lines)
        arrived = [sent[0]] + [shift_ia(sent[r], r & 3, r >> 2) for r in range(1, 8)]
        total = cycle_part(chunk, spots, me, cycle, arrived, total)

    cycle_sum = total.astype(jnp.bfloat16)
    half = lax.axis_size("ja") // 2
    partner = lax.ppermute(cycle_sum, "ja", [(b, b ^ half) for b in range(2 * half)])
    return finish(
        reverse % pairs,
        pno_count,
        occ_energy,
        exchange_ints,
        amps_masked,
        cycle_sum,
        partner,
        pno_energy,
    )


def solution(mesh):
    return jax.shard_map(
        local,
        mesh=mesh,
        in_specs=(
            P(AXES, None, None),
            P(AXES, None, None),
            P(AXES, None, None),
            P(AXES, None, None, None),
            P(AXES, None),
            P(AXES),
            P(AXES),
            P(AXES, None),
            P(AXES),
        ),
        out_specs=(P(AXES, None, None), P(AXES, None, None)),
        check_vma=False,
    )
```

```python
import functools

import jax
import jax.numpy as jnp
from jax import lax
from jax.experimental import pallas as pl
from jax.experimental.pallas import tpu as pltpu
from jax.sharding import PartitionSpec as P


RING = 4
AXES = ("ia", "ja")
CHUNKS = (
    ((0, 0), (0, 1), (0, 3), (3, 0)),
    ((1, 0), (3, 3), (1, 1), (3, 1)),
    ((1, 3), (0, 2), (3, 2), (1, 2)),
    ((2, 0), (2, 1), (2, 2), (2, 3)),
)
NOTES = 16
NT = (((1,), (1,)), ((), ()))


def ring_perm(stage, shift):
    pairs = []
    for i in range(2 * RING):
        for x in range(RING):
            for z in range(RING):
                if (i % 2 == 0) == (stage == 1):
                    there = (x + shift) % RING * RING + z
                else:
                    there = x * RING + (z + shift) % RING
                pairs.append((i * RING * RING + x * RING + z, i * RING * RING + there))
    return pairs


def shift_ja(value, stage, shift):
    return lax.ppermute(value, AXES, ring_perm(stage, shift))


def shift_ia(value, steps, flip):
    size = 2 * RING
    return lax.ppermute(
        value, "ia", [(i, (i // 2 + steps) % RING * 2 + (i % 2 ^ flip)) for i in range(size)]
    )


def owner_ja(core, x, z, u, t):
    dx = jnp.where(core == 0, t, u)
    dz = jnp.where(core == 0, u, t)
    return ((x + dx) & 3) * RING + ((z + dz) & 3)


def transform_kernel(chunk, starts, codes, me, *refs):
    blocks, lines = refs[:4], refs[4 : 4 + len(starts)]
    refs = refs[4 + len(starts) :]
    targets = refs[:8]
    owned, line_buf, result, own_sems, line_sems, out_sems = refs[8:]
    width = result.shape[-1]
    depth = owned.shape[2] - width
    rows = line_buf.shape[2]
    i, j = me[0], me[1]
    core, x, z = i & 1, j >> 2, j & 3

    def own(n):
        return pltpu.make_async_copy(blocks[n], owned.at[n], own_sems.at[n])

    def fetch(k, part, slot):
        source = lines[2 * k + part]
        return pltpu.make_async_copy(
            source.at[pl.ds(starts[2 * k + part], rows)],
            line_buf.at[slot, part],
            line_sems.at[slot, part],
        )

    def emit(k, slot):
        return pltpu.make_async_copy(result.at[slot], targets[k], out_sems.at[slot])

    for part in range(2):
        fetch(0, part, 0).start()
    for n in range(len(chunk)):
        own(n).start()
    for n in range(len(chunk)):
        own(n).wait()

    def reader(r, carry):
        slot = r & 1
        for k in range(1, 8):

            @pl.when(r + 1 == k)
            def _():
                for part in range(2):
                    fetch(k, part, k & 1).start()

        for part in range(2):
            fetch(0, part, slot).wait()

        @pl.when(r >= 2)
        def _():
            emit(0, slot).wait()

        inter, proj = [], []
        for n, (u, t) in enumerate(chunk):
            code = codes[r, i * 16 + owner_ja(core, x, z, u, t)]
            q = code & 7
            first, second = (code >> 3) & 7, code >> 6
            mine = jnp.concatenate(
                [
                    line_buf[slot, at >> 2, pl.ds(pl.multiple_of((at & 3) * width, width), width)]
                    for at in (first, second)
                ],
                axis=0,
            )
            inter.append(
                (
                    q,
                    jnp.dot(
                        mine, owned[n, q, :depth], preferred_element_type=jnp.float32
                    ).astype(jnp.bfloat16),
                )
            )
        for n, (q, value) in enumerate(inter):
            proj.append(
                jnp.dot(
                    value, owned[n, q, depth:], preferred_element_type=jnp.float32
                ).astype(jnp.bfloat16)
            )
        for n, (q, value) in enumerate(inter):
            for h in range(2):
                side = slice(h * width, (h + 1) * width)
                result[slot, n, h] = lax.dot_general(
                    proj[n][side], value[side], NT, preferred_element_type=jnp.float32
                ).astype(jnp.bfloat16)
        for k in range(8):

            @pl.when(r == k)
            def _():
                emit(k, k & 1).start()

        return carry

    lax.fori_loop(0, 8, reader, 0)
    for slot in range(2):
        emit(0, slot).wait()


def transform(chunk, codes, me, blocks, lines):
    pairs, rows, width = blocks[0].shape
    depth = rows - width
    smem = pl.BlockSpec(memory_space=pltpu.SMEM)
    hbm = pl.BlockSpec(memory_space=pltpu.HBM)
    shape = (len(chunk), 2, width, width)
    one = jax.ShapeDtypeStruct(shape, jnp.bfloat16)
    flops = 64 * 2 * width * width * (depth + 2 * width)
    return pl.pallas_call(
        functools.partial(transform_kernel, chunk, tuple(start for _, start in lines)),
        out_shape=[one] * 8,
        in_specs=[smem, smem] + [hbm] * (4 + len(lines)),
        out_specs=[hbm] * 8,
        scratch_shapes=[
            pltpu.VMEM((len(chunk),) + blocks[0].shape, jnp.bfloat16),
            pltpu.VMEM((2, 2, pairs // 2 * width, depth), jnp.bfloat16),
            pltpu.VMEM((2,) + shape, jnp.bfloat16),
            pltpu.SemaphoreType.DMA((len(chunk),)),
            pltpu.SemaphoreType.DMA((2, 2)),
            pltpu.SemaphoreType.DMA((2,)),
        ],
        compiler_params=pltpu.CompilerParams(vmem_limit_bytes=24 << 20),
        cost_estimate=pl.CostEstimate(
            flops=4 * flops, bytes_accessed=16 << 20, transcendentals=0
        ),
        name="transform",
    )(codes, me, *blocks, *[line for line, _ in lines])


def cycle_kernel(chunk, spots, me, cycle, *refs):
    arrived, before, total = refs[:8], refs[8], refs[9]
    values, sums, sems = refs[10:]
    i, j = me[0], me[1]
    y, core = i >> 1, i & 1
    x, z = j >> 2, j & 3

    copies = [
        pltpu.make_async_copy(arrived[r], values.at[r], sems.at[r]) for r in range(8)
    ]
    for copy in copies:
        copy.start()
    sums[...] = before[...]
    for r in range(8):
        other = core ^ (r >> 2)
        worker = ((y - (r & 3)) & 3) * 2 + other
        copies[r].wait()
        parts = []
        for n, (u, t) in enumerate(chunk):
            owner = worker * 16 + owner_ja(other, x, z, u, t)
            for h in range(2):
                spot = spots[h * 128 + owner]
                block = cycle[spot]
                value = values[r, n, h]
                part = jnp.dot(block, value, preferred_element_type=jnp.float32)
                part += lax.dot_general(value, block, NT, preferred_element_type=jnp.float32)
                parts.append((spot >> 5, part))
        for place, part in parts:
            sums[place] += part
    total[...] = sums[...].astype(total.dtype)


def cycle_part(chunk, spots, me, cycle, arrived, before, dtype):
    smem = pl.BlockSpec(memory_space=pltpu.SMEM)
    vmem = pl.BlockSpec(memory_space=pltpu.VMEM)
    hbm = pl.BlockSpec(memory_space=pltpu.HBM)
    width = cycle.shape[-1]
    return pl.pallas_call(
        functools.partial(cycle_kernel, chunk),
        out_shape=jax.ShapeDtypeStruct(before.shape, dtype),
        in_specs=[smem, smem, vmem] + [hbm] * 8 + [vmem],
        out_specs=vmem,
        scratch_shapes=[
            pltpu.VMEM((8,) + arrived[0].shape, jnp.bfloat16),
            pltpu.VMEM(before.shape, jnp.float32),
            pltpu.SemaphoreType.DMA((8,)),
        ],
        compiler_params=pltpu.CompilerParams(vmem_limit_bytes=20 << 20),
        cost_estimate=pl.CostEstimate(
            flops=4 * 64 * 4 * width**3, bytes_accessed=6 << 20, transcendentals=0
        ),
        name="cycle",
    )(spots, me, cycle, *arrived, before)


def prep_kernel(count, entries, amps, bases, block, line, masked, spots):
    p = pl.program_id(0)
    depth, width = bases.shape[1], bases.shape[2]
    pairs = pl.num_programs(0)
    cols = count[p]
    lane = lax.broadcasted_iota(jnp.int32, (depth, width), 1) < cols
    kept = jnp.where(lane, bases[0], jnp.zeros_like(bases[0]))
    block[0, :depth] = kept
    square = lane[:width] & (lax.broadcasted_iota(jnp.int32, (width, width), 0) < cols)
    kept_amps = jnp.where(square, amps[0], jnp.zeros_like(amps[0]))
    block[0, depth:] = kept_amps
    masked[0] = kept_amps
    line[pl.ds(pl.multiple_of(p * width, width), width)] = kept.T

    @pl.when(p == 0)
    def _():
        number = entries.shape[1]
        devices = spots.shape[1]
        row = jnp.broadcast_to(entries[...], (number, number))
        down = row.T
        at = lax.broadcasted_iota(jnp.int32, (number, number), 0)
        before = lax.broadcasted_iota(jnp.int32, (number, number), 1)
        same = ((row >> 3) == (down >> 3)) & (before < at)
        later = jnp.sum(same.astype(jnp.int32), axis=1, keepdims=True)
        named = (down[:, :devices] >> 3) == before[:, :devices]
        head = named & (later == 0)
        tail = named & (later == 1)
        place = at[:, :devices]
        zero = jnp.zeros_like(place)
        spot_head = jnp.sum(jnp.where(head, place, zero), axis=0, keepdims=True)
        spot_tail = jnp.sum(jnp.where(tail, place, zero), axis=0, keepdims=True)
        which = jnp.sum(jnp.where(head, down[:, :devices] & 7, zero), axis=0, keepdims=True)
        spots[0:1] = spot_head
        spots[1:2] = spot_tail
        row = lax.broadcasted_iota(jnp.int32, (NOTES, devices), 0)
        notes = jnp.where(row == 0, which, jnp.where(row == 1, spot_head >> 5, spot_tail >> 5))
        line[pl.ds(pairs * width, NOTES), :devices] = notes.astype(jnp.float32).astype(
            jnp.bfloat16
        )
        line[pl.ds(pairs * width, NOTES), devices:] = jnp.zeros(
            (NOTES, depth - devices), jnp.bfloat16
        )


def prep(count, entries, amps, bases):
    pairs, depth, width = bases.shape
    devices = entries.shape[1] // 2
    smem = pl.BlockSpec(memory_space=pltpu.SMEM)
    each = lambda *shape: pl.BlockSpec((1,) + shape, lambda p: (p, 0, 0))
    whole = lambda *shape: pl.BlockSpec(shape, lambda p: (0,) * len(shape))
    bf16 = jnp.bfloat16
    return pl.pallas_call(
        prep_kernel,
        grid=(pairs,),
        out_shape=(
            jax.ShapeDtypeStruct((pairs, depth + width, width), bf16),
            jax.ShapeDtypeStruct((pairs * width + NOTES, depth), bf16),
            jax.ShapeDtypeStruct(amps.shape, bf16),
            jax.ShapeDtypeStruct((2, devices), jnp.int32),
        ),
        in_specs=[smem, whole(1, 2 * devices), each(width, width), each(depth, width)],
        out_specs=(
            each(depth + width, width),
            whole(pairs * width + NOTES, depth),
            each(width, width),
            whole(2, devices),
        ),
        compiler_params=pltpu.CompilerParams(vmem_limit_bytes=16 << 20),
        cost_estimate=pl.CostEstimate(flops=0, bytes_accessed=5 << 20, transcendentals=0),
        name="prep",
    )(
        count,
        entries,
        pltpu.with_memory_space_constraint(amps, pltpu.HBM),
        pltpu.with_memory_space_constraint(bases, pltpu.HBM),
    )


def notes_kernel(ends, *refs):
    sources, codes, notes, sems = refs[:8], *refs[8:]
    devices = codes.shape[1]
    copies = [
        pltpu.make_async_copy(
            sources[r].at[pl.ds(ends[r], NOTES), pl.ds(0, devices)], notes.at[r], sems.at[r]
        )
        for r in range(8)
    ]
    for copy in copies:
        copy.start()
    for r in range(8):
        copies[r].wait()
        values = notes[r].astype(jnp.float32).astype(jnp.int32)
        codes[r : r + 1] = values[0:1] + 8 * values[1:2] + 64 * values[2:3]


def read_notes(lines, devices):
    hbm = pl.BlockSpec(memory_space=pltpu.HBM)
    ends = tuple(value.shape[0] - NOTES for value in lines)
    return pl.pallas_call(
        functools.partial(notes_kernel, ends),
        out_shape=jax.ShapeDtypeStruct((8, devices), jnp.int32),
        in_specs=[hbm] * 8,
        out_specs=pl.BlockSpec(memory_space=pltpu.VMEM),
        scratch_shapes=[
            pltpu.VMEM((8, NOTES, devices), jnp.bfloat16),
            pltpu.SemaphoreType.DMA((8,)),
        ],
        name="notes",
    )(*lines)


def finish_kernel(rev, count, occ, exchange, amps, own, partner, energy, new, res):
    pairs, width = amps.shape[0], amps.shape[1]
    row = lax.broadcasted_iota(jnp.int32, (width, width), 0)
    col = lax.broadcasted_iota(jnp.int32, (width, width), 1)
    for p in range(pairs):
        keep = (row < count[p]) & (col < count[p])
        mirrored = partner[rev[p]].astype(jnp.float32).T
        total = exchange[p].astype(jnp.float32) + own[p].astype(jnp.float32) + mirrored
        total = jnp.where(keep, total, 0.0)
        across = jnp.broadcast_to(energy[pl.ds(p, 1), :], (width, width))
        below = across.T + across - occ[p]
        res[p] = total
        updated = amps[p].astype(jnp.float32) - total / below
        new[p] = jnp.where(keep, updated, 0.0).astype(jnp.bfloat16)


def finish(rev, count, occ, exchange, amps, own, partner, energy):
    smem = pl.BlockSpec(memory_space=pltpu.SMEM)
    vmem = pl.BlockSpec(memory_space=pltpu.VMEM)
    return pl.pallas_call(
        finish_kernel,
        out_shape=(
            jax.ShapeDtypeStruct(amps.shape, jnp.bfloat16),
            jax.ShapeDtypeStruct(amps.shape, jnp.float32),
        ),
        in_specs=[smem] * 3 + [vmem] * 5,
        out_specs=(vmem, vmem),
        name="finish",
    )(rev, count, occ, exchange, amps, own, partner, energy)


def update(
    amplitudes,
    bases,
    exchange_ints,
    cycle_ints,
    pno_energy,
    occ_energy,
    pno_count,
    coupling,
    reverse,
):
    pairs, width = amplitudes.shape[0], amplitudes.shape[1]
    couple = coupling.shape[1]
    me = jnp.stack([lax.axis_index("ia"), lax.axis_index("ja")]).astype(jnp.int32)
    block, line, amps_masked, spots = prep(
        pno_count, coupling.reshape(1, -1), amplitudes, bases
    )
    devices = spots.shape[1]
    spots = spots.reshape(-1)
    half = line.shape[0] // 2 // width * width

    below = shift_ia(line, 1, 0)
    above = shift_ia(line, -1, 0)

    first = {0: block}
    first[3] = shift_ja(block, 1, 1)
    first[1] = shift_ja(block, 1, -1)
    held = {}
    held[3, 0] = shift_ja(block, 2, 1)
    held[1, 0] = shift_ja(block, 2, -1)

    far_a = shift_ia(below[:half], 1, 0)
    far_b = shift_ia(above[half:], -1, 0)
    block, first[1], first[3] = lax.optimization_barrier((block, first[1], first[3]))
    for t in (3, 1):
        held[3, t] = shift_ja(first[t], 2, 1)
    for t in (1, 3):
        held[1, t] = shift_ja(first[t], 2, -1)
    first[2] = shift_ja(block, 1, 2)
    near = []
    for value in (line, above, below):
        near.append(shift_ia(value, 0, 1))
    far = []
    for value in (far_a, far_b):
        far.append(shift_ia(value, 0, 1))

    def halves(value):
        return [(value, 0), (value, half)]

    lines = halves(line) + halves(above) + [(far_a, 0), (far_b, 0)] + halves(below)
    lines += halves(near[0]) + halves(near[1]) + [(far[0], 0), (far[1], 0)] + halves(near[2])
    codes = read_notes([lines[2 * r + 1][0] for r in range(8)], devices)
    for t in (0, 1, 3):
        held[0, t] = first[t]

    cycle = pltpu.with_memory_space_constraint(
        cycle_ints.reshape(pairs * couple, width, width), pltpu.VMEM
    )
    total = jnp.zeros((pairs, width, width), jnp.float32)
    arrivals = []
    for c, chunk in enumerate(CHUNKS):
        if c >= 2:
            total = cycle_part(
                CHUNKS[c - 2], spots, me, cycle, arrivals[c - 2], total, jnp.float32
            )
            codes, total = lax.optimization_barrier((codes, total))
        sent = transform(chunk, codes, me, [held[key] for key in chunk], lines)
        sent, total = lax.optimization_barrier((sent, total))
        if c == 0:
            held[0, 2] = first[2]
            for u, shift in ((3, 1), (1, -1)):
                held[u, 2] = shift_ja(first[2], 2, shift)
            for u, t, shift in ((3, 0, 1), (1, 1, -1), (3, 3, 1)):
                held[2, t] = shift_ja(held[u, t], 2, shift)
            held[2, 2] = shift_ja(first[2], 2, 2)
        back = [sent[0]]
        for r in range(1, 8):
            back.append(shift_ia(sent[r], r & 3, r >> 2))
        arrivals.append(back)
    total = cycle_part(CHUNKS[2], spots, me, cycle, arrivals[2], total, jnp.float32)
    cycle_sum = cycle_part(CHUNKS[3], spots, me, cycle, arrivals[3], total, jnp.bfloat16)
    apart = lax.axis_size("ja") // 2
    partner = lax.ppermute(cycle_sum, "ja", [(b, b ^ apart) for b in range(2 * apart)])
    return finish(
        reverse % pairs,
        pno_count,
        occ_energy,
        exchange_ints,
        amps_masked,
        cycle_sum,
        partner,
        pno_energy,
    )


def solution(mesh):
    return jax.shard_map(
        update,
        mesh=mesh,
        in_specs=(
            P(AXES, None, None),
            P(AXES, None, None),
            P(AXES, None, None),
            P(AXES, None, None, None),
            P(AXES, None),
            P(AXES),
            P(AXES),
            P(AXES, None),
            P(AXES),
        ),
        out_specs=(P(AXES, None, None), P(AXES, None, None)),
        check_vma=False,
    )
```

```python
import functools

import jax
import jax.numpy as jnp
from jax import lax
from jax.experimental import pallas as pl
from jax.experimental.pallas import tpu as pltpu
from jax.sharding import PartitionSpec as P


RING = 4
AXES = ("ia", "ja")
CHUNKS = (
    ((0, 0), (0, 1), (0, 3), (3, 0)),
    ((1, 0), (3, 3), (1, 1), (0, 2)),
    ((3, 1), (1, 3), (3, 2), (1, 2)),
    ((2, 0), (2, 1), (2, 3), (2, 2)),
)
NOTES = 16
NT = (((1,), (1,)), ((), ()))


def ring_perm(stage, shift):
    pairs = []
    for i in range(2 * RING):
        for x in range(RING):
            for z in range(RING):
                if (i % 2 == 0) == (stage == 1):
                    there = (x + shift) % RING * RING + z
                else:
                    there = x * RING + (z + shift) % RING
                pairs.append((i * RING * RING + x * RING + z, i * RING * RING + there))
    return pairs


def shift_ja(value, stage, shift):
    return lax.ppermute(value, AXES, ring_perm(stage, shift))


def shift_ia(value, steps, flip):
    size = 2 * RING
    return lax.ppermute(
        value, "ia", [(i, (i // 2 + steps) % RING * 2 + (i % 2 ^ flip)) for i in range(size)]
    )


def owner_ja(core, x, z, u, t):
    dx = jnp.where(core == 0, t, u)
    dz = jnp.where(core == 0, u, t)
    return ((x + dx) & 3) * RING + ((z + dz) & 3)


def transform_kernel(chunk, starts, codes, me, *refs):
    blocks, lines = refs[:4], refs[4 : 4 + len(starts)]
    refs = refs[4 + len(starts) :]
    targets = refs[:8]
    owned, line_buf, result, own_sems, line_sems, out_sems = refs[8:]
    width = result.shape[-1]
    depth = owned.shape[2] - width
    rows = line_buf.shape[2]
    i, j = me[0], me[1]
    core, x, z = i & 1, j >> 2, j & 3

    def own(n):
        return pltpu.make_async_copy(blocks[n], owned.at[n], own_sems.at[n])

    def fetch(k, part, slot):
        source = lines[2 * k + part]
        return pltpu.make_async_copy(
            source.at[pl.ds(starts[2 * k + part], rows)],
            line_buf.at[slot, part],
            line_sems.at[slot, part],
        )

    def emit(k, slot):
        return pltpu.make_async_copy(result.at[slot], targets[k], out_sems.at[slot])

    for part in range(2):
        fetch(0, part, 0).start()
    for n in range(len(chunk)):
        own(n).start()
    for n in range(len(chunk)):
        own(n).wait()

    def reader(r, carry):
        slot = r & 1
        for k in range(1, 8):

            @pl.when(r + 1 == k)
            def _():
                for part in range(2):
                    fetch(k, part, k & 1).start()

        for part in range(2):
            fetch(0, part, slot).wait()

        @pl.when(r >= 2)
        def _():
            emit(0, slot).wait()

        inter, proj = [], []
        for n, (u, t) in enumerate(chunk):
            code = codes[r, i * 16 + owner_ja(core, x, z, u, t)]
            q = code & 7
            first, second = (code >> 3) & 7, code >> 6
            mine = jnp.concatenate(
                [
                    line_buf[slot, at >> 2, pl.ds(pl.multiple_of((at & 3) * width, width), width)]
                    for at in (first, second)
                ],
                axis=0,
            )
            inter.append(
                (
                    q,
                    jnp.dot(
                        mine, owned[n, q, :depth], preferred_element_type=jnp.float32
                    ).astype(jnp.bfloat16),
                )
            )
        for n, (q, value) in enumerate(inter):
            proj.append(
                jnp.dot(
                    value, owned[n, q, depth:], preferred_element_type=jnp.float32
                ).astype(jnp.bfloat16)
            )
        for n, (q, value) in enumerate(inter):
            for h in range(2):
                side = slice(h * width, (h + 1) * width)
                result[slot, n, h] = lax.dot_general(
                    proj[n][side], value[side], NT, preferred_element_type=jnp.float32
                ).astype(jnp.bfloat16)
        for k in range(8):

            @pl.when(r == k)
            def _():
                emit(k, k & 1).start()

        return carry

    lax.fori_loop(0, 8, reader, 0)
    for slot in range(2):
        emit(0, slot).wait()


def transform(chunk, codes, me, blocks, lines):
    pairs, rows, width = blocks[0].shape
    depth = rows - width
    smem = pl.BlockSpec(memory_space=pltpu.SMEM)
    hbm = pl.BlockSpec(memory_space=pltpu.HBM)
    shape = (len(chunk), 2, width, width)
    one = jax.ShapeDtypeStruct(shape, jnp.bfloat16)
    flops = 64 * 2 * width * width * (depth + 2 * width)
    return pl.pallas_call(
        functools.partial(transform_kernel, chunk, tuple(start for _, start in lines)),
        out_shape=[one] * 8,
        in_specs=[smem, smem] + [hbm] * (4 + len(lines)),
        out_specs=[hbm] * 8,
        scratch_shapes=[
            pltpu.VMEM((len(chunk),) + blocks[0].shape, jnp.bfloat16),
            pltpu.VMEM((2, 2, pairs // 2 * width, depth), jnp.bfloat16),
            pltpu.VMEM((2,) + shape, jnp.bfloat16),
            pltpu.SemaphoreType.DMA((len(chunk),)),
            pltpu.SemaphoreType.DMA((2, 2)),
            pltpu.SemaphoreType.DMA((2,)),
        ],
        compiler_params=pltpu.CompilerParams(vmem_limit_bytes=24 << 20),
        cost_estimate=pl.CostEstimate(
            flops=4 * flops, bytes_accessed=16 << 20, transcendentals=0
        ),
        name="transform",
    )(codes, me, *blocks, *[line for line, _ in lines])


def cycle_kernel(chunk, spots, me, cycle, *refs):
    arrived, before, total = refs[:8], refs[8], refs[9]
    values, sums, sems = refs[10:]
    i, j = me[0], me[1]
    y, core = i >> 1, i & 1
    x, z = j >> 2, j & 3

    copies = [
        pltpu.make_async_copy(arrived[r], values.at[r], sems.at[r]) for r in range(8)
    ]
    for copy in copies:
        copy.start()
    sums[...] = before[...]
    for r in range(8):
        other = core ^ (r >> 2)
        worker = ((y - (r & 3)) & 3) * 2 + other
        copies[r].wait()
        parts = []
        for n, (u, t) in enumerate(chunk):
            owner = worker * 16 + owner_ja(other, x, z, u, t)
            for h in range(2):
                spot = spots[h * 128 + owner]
                block = cycle[spot]
                value = values[r, n, h]
                part = jnp.dot(block, value, preferred_element_type=jnp.float32)
                part += lax.dot_general(value, block, NT, preferred_element_type=jnp.float32)
                parts.append((spot >> 5, part))
        for place, part in parts:
            sums[place] += part
    total[...] = sums[...].astype(total.dtype)


def cycle_part(chunk, spots, me, cycle, arrived, before, dtype):
    smem = pl.BlockSpec(memory_space=pltpu.SMEM)
    vmem = pl.BlockSpec(memory_space=pltpu.VMEM)
    hbm = pl.BlockSpec(memory_space=pltpu.HBM)
    width = cycle.shape[-1]
    return pl.pallas_call(
        functools.partial(cycle_kernel, chunk),
        out_shape=jax.ShapeDtypeStruct(before.shape, dtype),
        in_specs=[smem, smem, vmem] + [hbm] * 8 + [vmem],
        out_specs=vmem,
        scratch_shapes=[
            pltpu.VMEM((8,) + arrived[0].shape, jnp.bfloat16),
            pltpu.VMEM(before.shape, jnp.float32),
            pltpu.SemaphoreType.DMA((8,)),
        ],
        compiler_params=pltpu.CompilerParams(vmem_limit_bytes=20 << 20),
        cost_estimate=pl.CostEstimate(
            flops=4 * 64 * 4 * width**3, bytes_accessed=6 << 20, transcendentals=0
        ),
        name="cycle",
    )(spots, me, cycle, *arrived, before)


def prep_kernel(count, entries, amps, bases, block, line, masked, spots):
    p = pl.program_id(0)
    depth, width = bases.shape[1], bases.shape[2]
    pairs = pl.num_programs(0)
    cols = count[p]
    lane = lax.broadcasted_iota(jnp.int32, (depth, width), 1) < cols
    kept = jnp.where(lane, bases[0], jnp.zeros_like(bases[0]))
    block[0, :depth] = kept
    square = lane[:width] & (lax.broadcasted_iota(jnp.int32, (width, width), 0) < cols)
    kept_amps = jnp.where(square, amps[0], jnp.zeros_like(amps[0]))
    block[0, depth:] = kept_amps
    masked[0] = kept_amps
    line[pl.ds(pl.multiple_of(p * width, width), width)] = kept.T

    @pl.when(p == 0)
    def _():
        number = entries.shape[1]
        devices = spots.shape[1]
        row = jnp.broadcast_to(entries[...], (number, number))
        down = row.T
        at = lax.broadcasted_iota(jnp.int32, (number, number), 0)
        before = lax.broadcasted_iota(jnp.int32, (number, number), 1)
        same = ((row >> 3) == (down >> 3)) & (before < at)
        later = jnp.sum(same.astype(jnp.int32), axis=1, keepdims=True)
        named = (down[:, :devices] >> 3) == before[:, :devices]
        head = named & (later == 0)
        tail = named & (later == 1)
        place = at[:, :devices]
        zero = jnp.zeros_like(place)
        spot_head = jnp.sum(jnp.where(head, place, zero), axis=0, keepdims=True)
        spot_tail = jnp.sum(jnp.where(tail, place, zero), axis=0, keepdims=True)
        which = jnp.sum(jnp.where(head, down[:, :devices] & 7, zero), axis=0, keepdims=True)
        spots[0:1] = spot_head
        spots[1:2] = spot_tail
        row = lax.broadcasted_iota(jnp.int32, (NOTES, devices), 0)
        notes = jnp.where(row == 0, which, jnp.where(row == 1, spot_head >> 5, spot_tail >> 5))
        line[pl.ds(pairs * width, NOTES), :devices] = notes.astype(jnp.float32).astype(
            jnp.bfloat16
        )
        line[pl.ds(pairs * width, NOTES), devices:] = jnp.zeros(
            (NOTES, depth - devices), jnp.bfloat16
        )


def prep(count, entries, amps, bases):
    pairs, depth, width = bases.shape
    devices = entries.shape[1] // 2
    smem = pl.BlockSpec(memory_space=pltpu.SMEM)
    each = lambda *shape: pl.BlockSpec((1,) + shape, lambda p: (p, 0, 0))
    whole = lambda *shape: pl.BlockSpec(shape, lambda p: (0,) * len(shape))
    bf16 = jnp.bfloat16
    return pl.pallas_call(
        prep_kernel,
        grid=(pairs,),
        out_shape=(
            jax.ShapeDtypeStruct((pairs, depth + width, width), bf16),
            jax.ShapeDtypeStruct((pairs * width + NOTES, depth), bf16),
            jax.ShapeDtypeStruct(amps.shape, bf16),
            jax.ShapeDtypeStruct((2, devices), jnp.int32),
        ),
        in_specs=[smem, whole(1, 2 * devices), each(width, width), each(depth, width)],
        out_specs=(
            each(depth + width, width),
            whole(pairs * width + NOTES, depth),
            each(width, width),
            whole(2, devices),
        ),
        compiler_params=pltpu.CompilerParams(vmem_limit_bytes=16 << 20),
        cost_estimate=pl.CostEstimate(flops=0, bytes_accessed=5 << 20, transcendentals=0),
        name="prep",
    )(
        count,
        entries,
        pltpu.with_memory_space_constraint(amps, pltpu.HBM),
        pltpu.with_memory_space_constraint(bases, pltpu.HBM),
    )


def notes_kernel(ends, *refs):
    sources, codes, notes, sems = refs[:8], *refs[8:]
    devices = codes.shape[1]
    copies = [
        pltpu.make_async_copy(
            sources[r].at[pl.ds(ends[r], NOTES), pl.ds(0, devices)], notes.at[r], sems.at[r]
        )
        for r in range(8)
    ]
    for copy in copies:
        copy.start()
    for r in range(8):
        copies[r].wait()
        values = notes[r].astype(jnp.float32).astype(jnp.int32)
        codes[r : r + 1] = values[0:1] + 8 * values[1:2] + 64 * values[2:3]


def read_notes(lines, devices):
    hbm = pl.BlockSpec(memory_space=pltpu.HBM)
    ends = tuple(value.shape[0] - NOTES for value in lines)
    return pl.pallas_call(
        functools.partial(notes_kernel, ends),
        out_shape=jax.ShapeDtypeStruct((8, devices), jnp.int32),
        in_specs=[hbm] * 8,
        out_specs=pl.BlockSpec(memory_space=pltpu.VMEM),
        scratch_shapes=[
            pltpu.VMEM((8, NOTES, devices), jnp.bfloat16),
            pltpu.SemaphoreType.DMA((8,)),
        ],
        compiler_params=pltpu.CompilerParams(vmem_limit_bytes=2 << 20),
        name="notes",
    )(*lines)


def finish_kernel(rev, count, occ, exchange, amps, own, partner, energy, new, res):
    pairs, width = amps.shape[0], amps.shape[1]
    row = lax.broadcasted_iota(jnp.int32, (width, width), 0)
    col = lax.broadcasted_iota(jnp.int32, (width, width), 1)
    for p in range(pairs):
        keep = (row < count[p]) & (col < count[p])
        mirrored = partner[rev[p]].astype(jnp.float32).T
        total = exchange[p].astype(jnp.float32) + own[p].astype(jnp.float32) + mirrored
        total = jnp.where(keep, total, 0.0)
        across = jnp.broadcast_to(energy[pl.ds(p, 1), :], (width, width))
        below = across.T + across - occ[p]
        res[p] = total
        updated = amps[p].astype(jnp.float32) - total / below
        new[p] = jnp.where(keep, updated, 0.0).astype(jnp.bfloat16)


def finish(rev, count, occ, exchange, amps, own, partner, energy):
    smem = pl.BlockSpec(memory_space=pltpu.SMEM)
    vmem = pl.BlockSpec(memory_space=pltpu.VMEM)
    return pl.pallas_call(
        finish_kernel,
        out_shape=(
            jax.ShapeDtypeStruct(amps.shape, jnp.bfloat16),
            jax.ShapeDtypeStruct(amps.shape, jnp.float32),
        ),
        in_specs=[smem] * 3 + [vmem] * 5,
        out_specs=(vmem, vmem),
        compiler_params=pltpu.CompilerParams(vmem_limit_bytes=12 << 20),
        name="finish",
    )(rev, count, occ, exchange, amps, own, partner, energy)


def update(
    amplitudes,
    bases,
    exchange_ints,
    cycle_ints,
    pno_energy,
    occ_energy,
    pno_count,
    coupling,
    reverse,
):
    pairs, width = amplitudes.shape[0], amplitudes.shape[1]
    couple = coupling.shape[1]
    me = jnp.stack([lax.axis_index("ia"), lax.axis_index("ja")]).astype(jnp.int32)
    block, line, amps_masked, spots = prep(
        pno_count, coupling.reshape(1, -1), amplitudes, bases
    )
    devices = spots.shape[1]
    spots = spots.reshape(-1)
    half = line.shape[0] // 2 // width * width

    below = shift_ia(line, 1, 0)
    above = shift_ia(line, -1, 0)

    first = {0: block}
    first[3] = shift_ja(block, 1, 1)
    first[1] = shift_ja(block, 1, -1)
    block, first[1], first[3] = lax.optimization_barrier((block, first[1], first[3]))
    held = {}
    for u, shift in ((3, 1), (1, -1)):
        held[u, 0] = shift_ja(block, 2, shift)
    first[2] = shift_ja(block, 1, 2)
    far_a = shift_ia(below[:half], 1, 0)
    far_b = shift_ia(above[half:], -1, 0)
    for u, t, shift in ((3, 3, 1), (1, 1, -1)):
        held[u, t] = shift_ja(first[t], 2, shift)
    for u, t, shift in ((3, 1, 1), (1, 3, -1)):
        held[u, t] = shift_ja(first[t], 2, shift)
    near = []
    for value in (line, above, below):
        near.append(shift_ia(value, 0, 1))
    far = []
    for value in (far_a, far_b):
        far.append(shift_ia(value, 0, 1))

    def halves(value):
        return [(value, 0), (value, half)]

    lines = halves(line) + halves(above) + [(far_a, 0), (far_b, 0)] + halves(below)
    lines += halves(near[0]) + halves(near[1]) + [(far[0], 0), (far[1], 0)] + halves(near[2])
    codes = read_notes([lines[2 * r + 1][0] for r in range(8)], devices)
    for t in (0, 1, 3):
        held[0, t] = first[t]

    cycle = pltpu.with_memory_space_constraint(
        cycle_ints.reshape(pairs * couple, width, width), pltpu.VMEM
    )
    total = jnp.zeros((pairs, width, width), jnp.float32)
    arrivals = []
    for c, chunk in enumerate(CHUNKS):
        if c >= 2:
            total = cycle_part(
                CHUNKS[c - 2], spots, me, cycle, arrivals[c - 2], total, jnp.float32
            )
            codes, total = lax.optimization_barrier((codes, total))
        sent = transform(chunk, codes, me, [held[key] for key in chunk], lines)
        sent, total = lax.optimization_barrier((sent, total))
        if c == 0:
            held[0, 2] = first[2]
            for u, shift in ((3, 1), (1, -1)):
                held[u, 2] = shift_ja(first[2], 2, shift)
            for u, t, shift in ((3, 0, 1), (1, 1, -1), (3, 3, 1), (1, 2, -1)):
                held[2, t] = shift_ja(held[u, t], 2, shift)
        back = [sent[0]]
        for r in range(1, 8):
            back.append(shift_ia(sent[r], r & 3, r >> 2))
        arrivals.append(back)
    total = cycle_part(CHUNKS[2], spots, me, cycle, arrivals[2], total, jnp.float32)
    cycle_sum = cycle_part(CHUNKS[3], spots, me, cycle, arrivals[3], total, jnp.bfloat16)
    apart = lax.axis_size("ja") // 2
    partner = lax.ppermute(cycle_sum, "ja", [(b, b ^ apart) for b in range(2 * apart)])
    return finish(
        reverse % pairs,
        pno_count,
        occ_energy,
        exchange_ints,
        amps_masked,
        cycle_sum,
        partner,
        pno_energy,
    )


def solution(mesh):
    return jax.shard_map(
        update,
        mesh=mesh,
        in_specs=(
            P(AXES, None, None),
            P(AXES, None, None),
            P(AXES, None, None),
            P(AXES, None, None, None),
            P(AXES, None),
            P(AXES),
            P(AXES),
            P(AXES, None),
            P(AXES),
        ),
        out_specs=(P(AXES, None, None), P(AXES, None, None)),
        check_vma=False,
    )
```

```python
import functools

import jax
import jax.numpy as jnp
from jax import lax
from jax.experimental import pallas as pl
from jax.experimental.pallas import tpu as pltpu
from jax.sharding import PartitionSpec as P


RING = 4
AXES = ("ia", "ja")
CHUNKS = (
    ((0, 0), (0, 1), (0, 3), (3, 0)),
    ((1, 0), (3, 3), (1, 1), (0, 2)),
    ((3, 1), (1, 3), (3, 2), (1, 2)),
    ((2, 0), (2, 1), (2, 3), (2, 2)),
)
NOTES = 16
NT = (((1,), (1,)), ((), ()))


def ring_perm(stage, shift):
    pairs = []
    for i in range(2 * RING):
        for x in range(RING):
            for z in range(RING):
                if (i % 2 == 0) == (stage == 1):
                    there = (x + shift) % RING * RING + z
                else:
                    there = x * RING + (z + shift) % RING
                pairs.append((i * RING * RING + x * RING + z, i * RING * RING + there))
    return pairs


def shift_ja(value, stage, shift):
    return lax.ppermute(value, AXES, ring_perm(stage, shift))


def shift_ia(value, steps, flip):
    size = 2 * RING
    return lax.ppermute(
        value, "ia", [(i, (i // 2 + steps) % RING * 2 + (i % 2 ^ flip)) for i in range(size)]
    )


def owner_ja(core, x, z, u, t):
    dx = jnp.where(core == 0, t, u)
    dz = jnp.where(core == 0, u, t)
    return ((x + dx) & 3) * RING + ((z + dz) & 3)


def transform_kernel(chunk, starts, codes, me, *refs):
    blocks, lines = refs[:4], refs[4 : 4 + len(starts)]
    refs = refs[4 + len(starts) :]
    targets = refs[:8]
    owned, line_buf, result, own_sems, line_sems, out_sems = refs[8:]
    width = result.shape[-1]
    depth = owned.shape[2] - width
    rows = line_buf.shape[2]
    i, j = me[0], me[1]
    core, x, z = i & 1, j >> 2, j & 3

    def own(n):
        return pltpu.make_async_copy(blocks[n], owned.at[n], own_sems.at[n])

    def fetch(k, part, slot):
        source = lines[2 * k + part]
        return pltpu.make_async_copy(
            source.at[pl.ds(starts[2 * k + part], rows)],
            line_buf.at[slot, part],
            line_sems.at[slot, part],
        )

    def emit(k, slot):
        return pltpu.make_async_copy(result.at[slot], targets[k], out_sems.at[slot])

    for part in range(2):
        fetch(0, part, 0).start()
    for n in range(len(chunk)):
        own(n).start()
    for n in range(len(chunk)):
        own(n).wait()

    def reader(r, carry):
        slot = r & 1
        for k in range(1, 8):

            @pl.when(r + 1 == k)
            def _():
                for part in range(2):
                    fetch(k, part, k & 1).start()

        for part in range(2):
            fetch(0, part, slot).wait()

        @pl.when(r >= 2)
        def _():
            emit(0, slot).wait()

        inter, proj = [], []
        for n, (u, t) in enumerate(chunk):
            code = codes[r, i * 16 + owner_ja(core, x, z, u, t)]
            q = code & 7
            first, second = (code >> 3) & 7, code >> 6
            mine = jnp.concatenate(
                [
                    line_buf[slot, at >> 2, pl.ds(pl.multiple_of((at & 3) * width, width), width)]
                    for at in (first, second)
                ],
                axis=0,
            )
            inter.append(
                (
                    q,
                    jnp.dot(
                        mine, owned[n, q, :depth], preferred_element_type=jnp.float32
                    ).astype(jnp.bfloat16),
                )
            )
        for n, (q, value) in enumerate(inter):
            proj.append(
                jnp.dot(
                    value, owned[n, q, depth:], preferred_element_type=jnp.float32
                ).astype(jnp.bfloat16)
            )
        for n, (q, value) in enumerate(inter):
            for h in range(2):
                side = slice(h * width, (h + 1) * width)
                result[slot, n, h] = lax.dot_general(
                    proj[n][side], value[side], NT, preferred_element_type=jnp.float32
                ).astype(jnp.bfloat16)
        for k in range(8):

            @pl.when(r == k)
            def _():
                emit(k, k & 1).start()

        return carry

    lax.fori_loop(0, 8, reader, 0)
    for slot in range(2):
        emit(0, slot).wait()


def transform(chunk, codes, me, blocks, lines):
    pairs, rows, width = blocks[0].shape
    depth = rows - width
    smem = pl.BlockSpec(memory_space=pltpu.SMEM)
    hbm = pl.BlockSpec(memory_space=pltpu.HBM)
    shape = (len(chunk), 2, width, width)
    one = jax.ShapeDtypeStruct(shape, jnp.bfloat16)
    flops = 64 * 2 * width * width * (depth + 2 * width)
    return pl.pallas_call(
        functools.partial(transform_kernel, chunk, tuple(start for _, start in lines)),
        out_shape=[one] * 8,
        in_specs=[smem, smem] + [hbm] * (4 + len(lines)),
        out_specs=[hbm] * 8,
        scratch_shapes=[
            pltpu.VMEM((len(chunk),) + blocks[0].shape, jnp.bfloat16),
            pltpu.VMEM((2, 2, pairs // 2 * width, depth), jnp.bfloat16),
            pltpu.VMEM((2,) + shape, jnp.bfloat16),
            pltpu.SemaphoreType.DMA((len(chunk),)),
            pltpu.SemaphoreType.DMA((2, 2)),
            pltpu.SemaphoreType.DMA((2,)),
        ],
        compiler_params=pltpu.CompilerParams(vmem_limit_bytes=24 << 20),
        cost_estimate=pl.CostEstimate(
            flops=4 * flops, bytes_accessed=16 << 20, transcendentals=0
        ),
        name="transform",
    )(codes, me, *blocks, *[line for line, _ in lines])


def cycle_kernel(chunk, readers, spots, me, cycle, *refs):
    number = len(readers)
    arrived, before, total = refs[:number], refs[number], refs[number + 1]
    values, sums, sems = refs[number + 2 :]
    i, j = me[0], me[1]
    y, core = i >> 1, i & 1
    x, z = j >> 2, j & 3

    copies = [
        pltpu.make_async_copy(arrived[k], values.at[k], sems.at[k]) for k in range(number)
    ]
    for copy in copies:
        copy.start()
    sums[...] = before[...]
    for k, r in enumerate(readers):
        other = core ^ (r >> 2)
        worker = ((y - (r & 3)) & 3) * 2 + other
        copies[k].wait()
        parts = []
        for n, (u, t) in enumerate(chunk):
            owner = worker * 16 + owner_ja(other, x, z, u, t)
            for h in range(2):
                spot = spots[h * 128 + owner]
                block = cycle[spot]
                value = values[k, n, h]
                part = jnp.dot(block, value, preferred_element_type=jnp.float32)
                part += lax.dot_general(value, block, NT, preferred_element_type=jnp.float32)
                parts.append((spot >> 5, part))
        for place, part in parts:
            sums[place] += part
    total[...] = sums[...].astype(total.dtype)


def cycle_part(chunk, spots, me, cycle, arrived, before, dtype, readers=tuple(range(8))):
    smem = pl.BlockSpec(memory_space=pltpu.SMEM)
    vmem = pl.BlockSpec(memory_space=pltpu.VMEM)
    hbm = pl.BlockSpec(memory_space=pltpu.HBM)
    width = cycle.shape[-1]
    return pl.pallas_call(
        functools.partial(cycle_kernel, chunk, readers),
        out_shape=jax.ShapeDtypeStruct(before.shape, dtype),
        in_specs=[smem, smem, vmem] + [hbm] * len(readers) + [vmem],
        out_specs=vmem,
        scratch_shapes=[
            pltpu.VMEM((len(readers),) + arrived[0].shape, jnp.bfloat16),
            pltpu.VMEM(before.shape, jnp.float32),
            pltpu.SemaphoreType.DMA((len(readers),)),
        ],
        compiler_params=pltpu.CompilerParams(vmem_limit_bytes=20 << 20),
        cost_estimate=pl.CostEstimate(
            flops=4 * 8 * len(readers) * 4 * width**3, bytes_accessed=6 << 20, transcendentals=0
        ),
        name="cycle",
    )(spots, me, cycle, *[arrived[r] for r in readers], before)


def prep_kernel(count, entries, amps, bases, block, line, masked, spots):
    p = pl.program_id(0)
    depth, width = bases.shape[1], bases.shape[2]
    pairs = pl.num_programs(0)
    cols = count[p]
    lane = lax.broadcasted_iota(jnp.int32, (depth, width), 1) < cols
    kept = jnp.where(lane, bases[0], jnp.zeros_like(bases[0]))
    block[0, :depth] = kept
    square = lane[:width] & (lax.broadcasted_iota(jnp.int32, (width, width), 0) < cols)
    kept_amps = jnp.where(square, amps[0], jnp.zeros_like(amps[0]))
    block[0, depth:] = kept_amps
    masked[0] = kept_amps
    line[pl.ds(pl.multiple_of(p * width, width), width)] = kept.T

    @pl.when(p == 0)
    def _():
        number = entries.shape[1]
        devices = spots.shape[1]
        row = jnp.broadcast_to(entries[...], (number, number))
        down = row.T
        at = lax.broadcasted_iota(jnp.int32, (number, number), 0)
        before = lax.broadcasted_iota(jnp.int32, (number, number), 1)
        same = ((row >> 3) == (down >> 3)) & (before < at)
        later = jnp.sum(same.astype(jnp.int32), axis=1, keepdims=True)
        named = (down[:, :devices] >> 3) == before[:, :devices]
        head = named & (later == 0)
        tail = named & (later == 1)
        place = at[:, :devices]
        zero = jnp.zeros_like(place)
        spot_head = jnp.sum(jnp.where(head, place, zero), axis=0, keepdims=True)
        spot_tail = jnp.sum(jnp.where(tail, place, zero), axis=0, keepdims=True)
        which = jnp.sum(jnp.where(head, down[:, :devices] & 7, zero), axis=0, keepdims=True)
        spots[0:1] = spot_head
        spots[1:2] = spot_tail
        row = lax.broadcasted_iota(jnp.int32, (NOTES, devices), 0)
        notes = jnp.where(row == 0, which, jnp.where(row == 1, spot_head >> 5, spot_tail >> 5))
        line[pl.ds(pairs * width, NOTES), :devices] = notes.astype(jnp.float32).astype(
            jnp.bfloat16
        )
        line[pl.ds(pairs * width, NOTES), devices:] = jnp.zeros(
            (NOTES, depth - devices), jnp.bfloat16
        )


def prep(count, entries, amps, bases):
    pairs, depth, width = bases.shape
    devices = entries.shape[1] // 2
    smem = pl.BlockSpec(memory_space=pltpu.SMEM)
    each = lambda *shape: pl.BlockSpec((1,) + shape, lambda p: (p, 0, 0))
    whole = lambda *shape: pl.BlockSpec(shape, lambda p: (0,) * len(shape))
    bf16 = jnp.bfloat16
    return pl.pallas_call(
        prep_kernel,
        grid=(pairs,),
        out_shape=(
            jax.ShapeDtypeStruct((pairs, depth + width, width), bf16),
            jax.ShapeDtypeStruct((pairs * width + NOTES, depth), bf16),
            jax.ShapeDtypeStruct(amps.shape, bf16),
            jax.ShapeDtypeStruct((2, devices), jnp.int32),
        ),
        in_specs=[smem, whole(1, 2 * devices), each(width, width), each(depth, width)],
        out_specs=(
            each(depth + width, width),
            whole(pairs * width + NOTES, depth),
            each(width, width),
            whole(2, devices),
        ),
        compiler_params=pltpu.CompilerParams(vmem_limit_bytes=16 << 20),
        cost_estimate=pl.CostEstimate(flops=0, bytes_accessed=5 << 20, transcendentals=0),
        name="prep",
    )(
        count,
        entries,
        pltpu.with_memory_space_constraint(amps, pltpu.HBM),
        pltpu.with_memory_space_constraint(bases, pltpu.HBM),
    )


def notes_kernel(ends, *refs):
    sources, codes, notes, sems = refs[:8], *refs[8:]
    devices = codes.shape[1]
    copies = [
        pltpu.make_async_copy(
            sources[r].at[pl.ds(ends[r], NOTES), pl.ds(0, devices)], notes.at[r], sems.at[r]
        )
        for r in range(8)
    ]
    for copy in copies:
        copy.start()
    for r in range(8):
        copies[r].wait()
        values = notes[r].astype(jnp.float32).astype(jnp.int32)
        codes[r : r + 1] = values[0:1] + 8 * values[1:2] + 64 * values[2:3]


def read_notes(lines, devices):
    hbm = pl.BlockSpec(memory_space=pltpu.HBM)
    ends = tuple(value.shape[0] - NOTES for value in lines)
    return pl.pallas_call(
        functools.partial(notes_kernel, ends),
        out_shape=jax.ShapeDtypeStruct((8, devices), jnp.int32),
        in_specs=[hbm] * 8,
        out_specs=pl.BlockSpec(memory_space=pltpu.VMEM),
        scratch_shapes=[
            pltpu.VMEM((8, NOTES, devices), jnp.bfloat16),
            pltpu.SemaphoreType.DMA((8,)),
        ],
        compiler_params=pltpu.CompilerParams(vmem_limit_bytes=2 << 20),
        name="notes",
    )(*lines)


def finish_kernel(rev, count, occ, exchange, amps, own, partner, energy, new, res):
    pairs, width = amps.shape[0], amps.shape[1]
    row = lax.broadcasted_iota(jnp.int32, (width, width), 0)
    col = lax.broadcasted_iota(jnp.int32, (width, width), 1)
    for p in range(pairs):
        keep = (row < count[p]) & (col < count[p])
        mirrored = partner[rev[p]].astype(jnp.float32).T
        total = exchange[p].astype(jnp.float32) + own[p].astype(jnp.float32) + mirrored
        total = jnp.where(keep, total, 0.0)
        across = jnp.broadcast_to(energy[pl.ds(p, 1), :], (width, width))
        below = across.T + across - occ[p]
        res[p] = total
        updated = amps[p].astype(jnp.float32) - total / below
        new[p] = jnp.where(keep, updated, 0.0).astype(jnp.bfloat16)


def finish(rev, count, occ, exchange, amps, own, partner, energy):
    smem = pl.BlockSpec(memory_space=pltpu.SMEM)
    vmem = pl.BlockSpec(memory_space=pltpu.VMEM)
    return pl.pallas_call(
        finish_kernel,
        out_shape=(
            jax.ShapeDtypeStruct(amps.shape, jnp.bfloat16),
            jax.ShapeDtypeStruct(amps.shape, jnp.float32),
        ),
        in_specs=[smem] * 3 + [vmem] * 5,
        out_specs=(vmem, vmem),
        compiler_params=pltpu.CompilerParams(vmem_limit_bytes=12 << 20),
        name="finish",
    )(rev, count, occ, exchange, amps, own, partner, energy)


def update(
    amplitudes,
    bases,
    exchange_ints,
    cycle_ints,
    pno_energy,
    occ_energy,
    pno_count,
    coupling,
    reverse,
):
    pairs, width = amplitudes.shape[0], amplitudes.shape[1]
    couple = coupling.shape[1]
    me = jnp.stack([lax.axis_index("ia"), lax.axis_index("ja")]).astype(jnp.int32)
    block, line, amps_masked, spots = prep(
        pno_count, coupling.reshape(1, -1), amplitudes, bases
    )
    devices = spots.shape[1]
    spots = spots.reshape(-1)
    half = line.shape[0] // 2 // width * width

    below = shift_ia(line, 1, 0)
    above = shift_ia(line, -1, 0)

    first = {0: block}
    first[3] = shift_ja(block, 1, 1)
    first[1] = shift_ja(block, 1, -1)
    block, first[1], first[3] = lax.optimization_barrier((block, first[1], first[3]))
    held = {}
    for u, shift in ((3, 1), (1, -1)):
        held[u, 0] = shift_ja(block, 2, shift)
    first[2] = shift_ja(block, 1, 2)
    far_a = shift_ia(below[:half], 1, 0)
    far_b = shift_ia(above[half:], -1, 0)
    for u, t, shift in ((3, 3, 1), (1, 1, -1)):
        held[u, t] = shift_ja(first[t], 2, shift)
    for u, t, shift in ((3, 1, 1), (1, 3, -1)):
        held[u, t] = shift_ja(first[t], 2, shift)
    near = []
    for value in (line, above, below):
        near.append(shift_ia(value, 0, 1))
    far = []
    for value in (far_a, far_b):
        far.append(shift_ia(value, 0, 1))

    def halves(value):
        return [(value, 0), (value, half)]

    lines = halves(line) + halves(above) + [(far_a, 0), (far_b, 0)] + halves(below)
    lines += halves(near[0]) + halves(near[1]) + [(far[0], 0), (far[1], 0)] + halves(near[2])
    codes = read_notes([lines[2 * r + 1][0] for r in range(8)], devices)
    for t in (0, 1, 3):
        held[0, t] = first[t]

    cycle = pltpu.with_memory_space_constraint(
        cycle_ints.reshape(pairs * couple, width, width), pltpu.VMEM
    )
    total = jnp.zeros((pairs, width, width), jnp.float32)
    arrivals = []
    for c, chunk in enumerate(CHUNKS):
        if c >= 2:
            total = cycle_part(CHUNKS[c - 2], spots, me, cycle, arrivals[c - 2], total, jnp.float32)
            codes, total = lax.optimization_barrier((codes, total))
        sent = transform(chunk, codes, me, [held[key] for key in chunk], lines)
        sent, total = lax.optimization_barrier((sent, total))
        if c == 0:
            held[0, 2] = first[2]
            for u, shift in ((3, 1), (1, -1)):
                held[u, 2] = shift_ja(first[2], 2, shift)
            for u, t, shift in ((3, 0, 1), (1, 1, -1), (3, 3, 1), (1, 2, -1)):
                held[2, t] = shift_ja(held[u, t], 2, shift)
        back = [sent[0]]
        for r in range(1, 8):
            back.append(shift_ia(sent[r], r & 3, r >> 2))
        arrivals.append(back)
    total = cycle_part(CHUNKS[2], spots, me, cycle, arrivals[2], total, jnp.float32)
    total = cycle_part(
        CHUNKS[3], spots, me, cycle, arrivals[3], total, jnp.float32, tuple(range(7))
    )
    cycle_sum = cycle_part(CHUNKS[3], spots, me, cycle, arrivals[3], total, jnp.bfloat16, (7,))
    apart = lax.axis_size("ja") // 2
    partner = lax.ppermute(cycle_sum, "ja", [(b, b ^ apart) for b in range(2 * apart)])
    return finish(
        reverse % pairs,
        pno_count,
        occ_energy,
        exchange_ints,
        amps_masked,
        cycle_sum,
        partner,
        pno_energy,
    )


def solution(mesh):
    return jax.shard_map(
        update,
        mesh=mesh,
        in_specs=(
            P(AXES, None, None),
            P(AXES, None, None),
            P(AXES, None, None),
            P(AXES, None, None, None),
            P(AXES, None),
            P(AXES),
            P(AXES),
            P(AXES, None),
            P(AXES),
        ),
        out_specs=(P(AXES, None, None), P(AXES, None, None)),
        check_vma=False,
    )
```
